512 devices in a mesh: group: 32 (over x, z), local: 16 (over y, core).
Axes of the slice: x: 4, y: 8, z: 8, core: 2. Of those that a mesh axis runs over, the one named last changes fastest.
Arguments:
- tokens: bfloat16 [4096, 3584], P(('group', 'local')), may hold values from -6 to 6
- routes: int32 [4096, 8], P(('group', 'local')), may hold values from 0 to 127, as said below
- route_gates: float32 [4096, 8], P(('group', 'local')), may hold values from 0.2 to 2
- gate_weight: bfloat16 [512, 3584, 256], P(('group', 'local')), may hold values from -0.09375 to 0.09375
- up_weight: bfloat16 [512, 3584, 256], P(('group', 'local')), may hold values from -0.09375 to 0.09375
Outputs:
- routed_hidden: bfloat16 [512, 1024, 256], P(('group', 'local'))
The draws below stay inside these ranges and needn't reach their ends.
Inputs may be any that keep to these rules, and one draw needn't show every extreme that they name: `routes`: each token names 8 different experts, lying in exactly 4 of the 8 expert groups of 16 consecutive experts; in each aligned block of 4 tokens every block of 4 consecutive experts is used by exactly one token, which names 1 of its experts.
All inputs are finite; a program needn't handle non-finite values.
Results may differ from the reference program's by a relative error of at most 0.012.
Values may be sent and summed in bfloat16 or wider, within the bound.
No kernel may reach another device: no remote copies, remote signals or barrier semaphores. Data moves between devices by JAX's collectives and lax.ppermute only.
A program may use at most 64 MiB of HBM per device.

```python
import math
import jax
import jax.numpy as jnp
from jax import lax

D = 3584
FF = 1024
NEG = 8
EXP_MESH = 4
TOPG = 4
TOP = 8
SPLIT = 4
FF_DEV = 256
EXPERTS = 128
QPG = 4
PQ = 2
MT = 8
PICKS = 1
TOKENS = 4096
BLOCK = 4
ROWS = 1024
N_GROUP = 32


def draw_routes(key, part):
    base_key = jax.random.fold_in(key, 11)
    key_groups, key_quarters, key_bias, key_favour, key_noise = jax.random.split(base_key, 5)
    block_count = TOKENS // BLOCK
    sets_each = QPG // PQ
    group_scores = jax.random.randint(key_groups, (block_count, NEG), 0, 2 ** 20) * NEG + jnp.arange(NEG, dtype=jnp.int32)[None, :]
    group_order = jnp.argsort(group_scores, axis=1).astype(jnp.int32)
    quarter_scores = jax.random.randint(key_quarters, (block_count, NEG, QPG), 0, 2 ** 20) * QPG + jnp.arange(QPG, dtype=jnp.int32)[None, None, :]
    quarter_order = jnp.argsort(quarter_scores, axis=2).astype(jnp.int32)
    set_index = jnp.arange(BLOCK, dtype=jnp.int32)[:, None] + BLOCK * jnp.arange(TOPG, dtype=jnp.int32)[None, :]
    position = set_index // sets_each
    part_index = set_index % sets_each
    group_of = group_order[:, position]
    quarter_rows = quarter_order[:, position]
    quarter_pick = part_index[:, :, None] * PQ + jnp.arange(PQ, dtype=jnp.int32)[None, None, :]
    quarter_pick = jnp.broadcast_to(quarter_pick[None], (block_count, BLOCK, TOPG, PQ))
    quarters = jnp.take_along_axis(quarter_rows, quarter_pick, axis=3)
    blocks_used = (group_of[:, :, :, None] * QPG + quarters).reshape(TOKENS, MT)
    candidates = blocks_used[:, :, None] * EXP_MESH + jnp.arange(EXP_MESH, dtype=jnp.int32)[None, None, :]
    expert_bias = jax.random.randint(key_bias, (EXPERTS,), 0, 3000)
    hot_expert = jax.random.randint(key_favour, (), 0, EXPERTS)
    expert_bias = expert_bias + jnp.where(jnp.arange(EXPERTS, dtype=jnp.int32) == hot_expert, 1000000, 0)
    noise_draw = jax.random.randint(key_noise, candidates.shape, 0, 3000)
    scores = (noise_draw + expert_bias[candidates]) * EXP_MESH + jnp.arange(EXP_MESH, dtype=jnp.int32)[None, None, :]
    _, picked = lax.top_k(scores, PICKS)
    chosen = jnp.take_along_axis(candidates, picked, axis=2)
    return chosen.reshape(TOKENS, TOP).astype(jnp.int32)


def shard_levels(key, extent, pieces, smallest, largest):
    loudness = 1.0
    for dim, blocks in pieces:
        heights = jax.random.uniform(jax.random.fold_in(jax.random.fold_in(key, 6), dim), (blocks,), jnp.float32, smallest / len(pieces), largest / len(pieces))
        loudness = loudness * jnp.repeat(jnp.exp(heights), extent[dim] // blocks).reshape((-1,) + (1,) * (len(extent) - 1 - dim))
    return loudness


def bell_draw(key, extent, width, most, cuts=(), held_as=jnp.bfloat16):
    entries = width * jax.random.normal(key, extent, jnp.float32)
    if cuts:
        entries = entries * shard_levels(key, extent, cuts, -0.22, 0.18)
    return jnp.clip(entries, -most, most).astype(held_as)


def setup_inputs(seed: int = 0) -> dict:
    key_of = jax.random.split(jax.random.key(seed), 6)
    tokens = bell_draw(key_of[0], (TOKENS, D), 1.0, 6.0, ((0, 512),))
    routes = draw_routes(jax.random.fold_in(key_of[5], 71), 0)
    route_gates = jnp.clip(jnp.exp(math.log(2.0) - 2.3025851 * jax.random.uniform(key_of[2], (TOKENS, TOP), jnp.float32) ** shard_levels(key_of[2], (TOKENS, TOP), ((0, 512),), -0.2, 0.2)), 0.2, 2.0)
    gate_weight = bell_draw(key_of[3], (EXPERTS * SPLIT, D, FF_DEV), D ** -0.5, 0.09375, ((0, 512),))
    up_weight = bell_draw(key_of[4], (EXPERTS * SPLIT, D, FF_DEV), D ** -0.5, 0.09375, ((0, 512),))
    return dict(tokens=tokens, routes=routes, route_gates=route_gates, gate_weight=gate_weight, up_weight=up_weight)


def one_group(group_index, tokens, routes, route_gates, gate_weight, up_weight):
    member = jnp.any(routes // EXP_MESH == group_index, axis=1)
    row_order = jnp.argsort(jnp.where(member, 0, 1).astype(jnp.int32), stable=True)[:ROWS]
    token_rows = tokens[row_order]
    chosen_routes = routes[row_order]
    chosen_gates = route_gates[row_order]
    pieces_out = []
    for slot_index in range(EXP_MESH):
        expert = group_index * EXP_MESH + slot_index
        weight = jnp.sum(jnp.where(chosen_routes == expert, chosen_gates, jnp.zeros_like(chosen_gates)), axis=1)
        start_block = (expert * SPLIT).astype(jnp.int32)
        gate_block = lax.dynamic_slice_in_dim(gate_weight, start_block, SPLIT, 0)
        up_block = lax.dynamic_slice_in_dim(up_weight, start_block, SPLIT, 0)
        gate_full = jnp.transpose(gate_block, (1, 0, 2)).reshape(D, FF)
        up_full = jnp.transpose(up_block, (1, 0, 2)).reshape(D, FF)
        pre_gate = jnp.dot(token_rows, gate_full, preferred_element_type=jnp.float32)
        pre_up = jnp.dot(token_rows, up_full, preferred_element_type=jnp.float32)
        hidden = (jax.nn.silu(pre_gate) * pre_up * weight[:, None]).astype(jnp.bfloat16)
        pieces_out.append(jnp.transpose(hidden.reshape(ROWS, SPLIT, FF_DEV), (1, 0, 2)))
    return jnp.concatenate(pieces_out, axis=0)


def reference(tokens, routes, route_gates, gate_weight, up_weight):
    def per_group(group_index):
        return one_group(group_index, tokens, routes, route_gates, gate_weight, up_weight)

    stacked = lax.map(per_group, jnp.arange(N_GROUP, dtype=jnp.int32))
    return stacked.reshape(EXPERTS * SPLIT, ROWS, FF_DEV)
```

```python
import jax
import jax.numpy as jnp
from jax import lax
from jax.experimental import pallas as pl
from jax.experimental.pallas import tpu as pltpu
from jax.sharding import PartitionSpec as P

EXP_MESH = 4
BLOCK = 4
GATE_ONE = 16000.0
CODE_MAX = 32000.0
EXP_BIAS = 200.0


def pack_kernel(tokens_ref, routes_ref, gates_ref, out_ref):
    count, width = tokens_ref.shape
    rows = out_ref.shape[0]
    per_group = count // BLOCK
    experts = out_ref.shape[1] - width
    tok = tokens_ref[...].astype(jnp.float32)
    largest = jnp.maximum(jnp.max(jnp.abs(tok), axis=1, keepdims=True), 1e-25)
    power = jnp.floor(jnp.log2(CODE_MAX / largest))
    codes = jnp.round(tok * jnp.exp2(power))
    routes = routes_ref[...]
    gate_codes = jnp.round(gates_ref[...] * GATE_ONE)
    expert = lax.broadcasted_iota(jnp.int32, (count, experts), 1)
    row = lax.broadcasted_iota(jnp.int32, (count, rows), 1)
    token = lax.broadcasted_iota(jnp.int32, (count, rows), 0)
    side = jnp.zeros((count, experts), jnp.float32)
    chosen = jnp.zeros((count, rows), jnp.float32)
    for k in range(routes.shape[1]):
        route = routes[:, k : k + 1]
        side = side + jnp.where(expert == route, gate_codes[:, k : k + 1], 0.0)
        chosen = jnp.where(route // EXP_MESH == row // per_group, 1.0, chosen)
    side = jnp.where(side > 0.0, side, -(power + EXP_BIAS))
    chosen = jnp.where(token // BLOCK == row % per_group, chosen, 0.0)
    chosen = chosen.T.astype(jnp.bfloat16)

    def send(values, first, size):
        high = jnp.floor(values * (1.0 / 256.0))
        low = values - 256.0 * high
        picked = jnp.dot(chosen, (256.0 * high).astype(jnp.bfloat16), preferred_element_type=jnp.float32)
        picked += jnp.dot(chosen, low.astype(jnp.bfloat16), preferred_element_type=jnp.float32)
        out_ref[:, first : first + size] = picked.astype(jnp.int32).astype(jnp.int16)

    send(codes, 0, width)
    send(side, width, experts)


def pack_rows(tokens, routes, route_gates, n_group, experts):
    count, width = tokens.shape
    rows = n_group * (count // BLOCK)
    return pl.pallas_call(
        pack_kernel,
        out_shape=jax.ShapeDtypeStruct((rows, width + experts), jnp.int16),
        in_specs=[pl.BlockSpec(memory_space=pltpu.VMEM)] * 3,
        out_specs=pl.BlockSpec(memory_space=pltpu.VMEM),
    )(tokens, routes, route_gates)


def shards(tokens, routes, route_gates, gate_weight, up_weight):
    n_group = lax.axis_size("group")
    n_local = lax.axis_size("local")
    n_y = n_local // 2
    width = tokens.shape[1]
    experts = n_group * EXP_MESH
    per_group = tokens.shape[0] // BLOCK
    local = lax.axis_index("local")
    core = local % 2
    my_expert = lax.axis_index("group") * EXP_MESH + local // (n_local // EXP_MESH)
    swap = [(2 * y + c, 2 * y + 1 - c) for y in range(n_y) for c in range(2)]
    same_core = [[2 * y + c for y in range(n_y)] for c in range(2)]

    other_gate = lax.ppermute(gate_weight, "local", swap)
    other_up = lax.ppermute(up_weight, "local", swap)

    packed = pack_rows(tokens, routes, route_gates, n_group, experts)
    packed = packed.reshape(n_group, per_group, width + experts)
    received = lax.all_to_all(packed, "group", split_axis=0, concat_axis=0, tiled=True)
    received = received.reshape(1, n_group * per_group, width + experts)
    gathered = lax.all_gather(received, "local", axis=0, axis_index_groups=same_core, tiled=True)
    gathered = gathered.reshape(-1, width + experts)

    rows = gathered[:, :width].astype(jnp.bfloat16)
    side = gathered[:, width:].astype(jnp.float32)
    scale = jnp.exp2(jnp.min(side, axis=1, keepdims=True) + EXP_BIAS)
    mine = lax.broadcasted_iota(jnp.int32, (1, experts), 1) == my_expert
    weight = jnp.sum(jnp.where(mine, jnp.maximum(side, 0.0), 0.0), axis=1, keepdims=True)
    weight = weight * (1.0 / GATE_ONE)

    def hidden(gate, up):
        pre_gate = jnp.dot(rows, gate[0], preferred_element_type=jnp.float32) * scale
        pre_up = jnp.dot(rows, up[0], preferred_element_type=jnp.float32) * scale
        return (jax.nn.silu(pre_gate) * pre_up * weight).astype(jnp.bfloat16)

    for_other = hidden(other_gate, other_up)
    from_other = lax.ppermute(for_other, "local", swap)
    own = hidden(gate_weight, up_weight)
    out_dim = own.shape[-1]

    first = jnp.where(core == 0, own, from_other).reshape(n_y, n_group, 1, per_group, out_dim)
    second = jnp.where(core == 0, from_other, own).reshape(n_y, n_group, 1, per_group, out_dim)
    both = jnp.concatenate([first, second], axis=2)
    return jnp.transpose(both, (1, 0, 2, 3, 4)).reshape(1, -1, out_dim)


def solution(mesh):
    placed = (
        P(("group", "local"), None),
        P(("group", "local"), None),
        P(("group", "local"), None),
        P(("group", "local"), None, None),
        P(("group", "local"), None, None),
    )
    return jax.shard_map(
        shards,
        mesh=mesh,
        in_specs=placed,
        out_specs=P(("group", "local"), None, None),
        check_vma=False,
    )
```

```python
import functools

import jax
import jax.numpy as jnp
from jax import lax
from jax.experimental import pallas as pl
from jax.experimental.pallas import tpu as pltpu
from jax.sharding import PartitionSpec as P

EXP_MESH = 4
BLOCK = 4
LANES = 128
GATE_ONE = 16000.0
CODE_MAX = 32000.0
EXP_BIAS = 200.0


def pack_kernel(tokens_ref, routes_ref, gates_ref, out_ref):
    count, width = tokens_ref.shape
    n_group, per_group, packed_width = out_ref.shape
    rows = n_group * per_group
    experts = packed_width - width
    tok = tokens_ref[...].astype(jnp.float32)
    largest = jnp.maximum(jnp.max(jnp.abs(tok), axis=1, keepdims=True), 1e-25)
    power = jnp.floor(jnp.log2(CODE_MAX / largest))
    codes = jnp.round(tok * jnp.exp2(power))
    routes = routes_ref[...]
    gate_codes = jnp.round(gates_ref[...] * GATE_ONE)
    expert = lax.broadcasted_iota(jnp.int32, (count, experts), 1)
    row = lax.broadcasted_iota(jnp.int32, (count, rows), 1)
    token = lax.broadcasted_iota(jnp.int32, (count, rows), 0)
    side = jnp.zeros((count, experts), jnp.float32)
    chosen = jnp.zeros((count, rows), jnp.float32)
    for k in range(routes.shape[1]):
        route = routes[:, k : k + 1]
        side = side + jnp.where(expert == route, gate_codes[:, k : k + 1], 0.0)
        chosen = jnp.where(route // EXP_MESH == row // per_group, 1.0, chosen)
    side = jnp.where(side > 0.0, side, -(power + EXP_BIAS))
    chosen = jnp.where(token // BLOCK == row % per_group, chosen, 0.0)
    chosen = chosen.T.astype(jnp.bfloat16)

    def send(values, first, size):
        high = jnp.floor(values * (1.0 / 256.0))
        low = values - 256.0 * high
        picked = jnp.dot(chosen, (256.0 * high).astype(jnp.bfloat16), preferred_element_type=jnp.float32)
        picked += jnp.dot(chosen, low.astype(jnp.bfloat16), preferred_element_type=jnp.float32)
        picked = picked.astype(jnp.int32).astype(jnp.int16)
        for group in range(n_group):
            out_ref[group, :, first : first + size] = picked[group * per_group : (group + 1) * per_group]

    send(codes, 0, width)
    send(side, width, experts)


def pack_rows(tokens, routes, route_gates, n_group, experts):
    count, width = tokens.shape
    return pl.pallas_call(
        pack_kernel,
        out_shape=jax.ShapeDtypeStruct((n_group, count // BLOCK, width + experts), jnp.int16),
        in_specs=[pl.BlockSpec(memory_space=pltpu.VMEM)] * 3,
        out_specs=pl.BlockSpec(memory_space=pltpu.VMEM),
    )(tokens, routes, route_gates)


def hidden_kernel(expert_ref, codes_ref, *refs):
    weights, (other_ref, own_ref), (rows, held, arrived) = refs[:4], refs[4:6], refs[6:]
    width = rows.shape[1]
    copies = [pltpu.make_async_copy(weights[j], held.at[j], arrived.at[j]) for j in range(4)]
    for copy in copies:
        copy.start()
    rows[...] = codes_ref[:, :width].astype(jnp.float32).astype(jnp.bfloat16)
    side = codes_ref[:, width:].astype(jnp.float32)
    lane = lax.broadcasted_iota(jnp.int32, side.shape, 1)
    weight = jnp.sum(jnp.where(lane == expert_ref[0], jnp.maximum(side, 0.0), 0.0), axis=1, keepdims=True)
    weight = weight * (1.0 / GATE_ONE)
    scale = jnp.exp2(jnp.min(side, axis=1, keepdims=True) + EXP_BIAS)
    for first, out_ref in ((0, other_ref), (2, own_ref)):
        copies[first].wait()
        pre_gate = jnp.dot(rows[...], held[first], preferred_element_type=jnp.float32) * scale
        copies[first + 1].wait()
        pre_up = jnp.dot(rows[...], held[first + 1], preferred_element_type=jnp.float32) * scale
        out_ref[...] = (pre_gate / (1.0 + jnp.exp(-pre_gate)) * pre_up * weight).astype(out_ref.dtype)


def multiply(expert, codes, width, weights):
    count = codes.shape[0]
    depth, out_dim = weights[0].shape
    return pl.pallas_call(
        hidden_kernel,
        out_shape=[jax.ShapeDtypeStruct((count, out_dim), jnp.bfloat16)] * 2,
        in_specs=[pl.BlockSpec(memory_space=pltpu.SMEM), pl.BlockSpec(memory_space=pltpu.VMEM)]
        + [pl.BlockSpec(memory_space=pl.ANY)] * 4,
        out_specs=[pl.BlockSpec(memory_space=pltpu.VMEM)] * 2,
        scratch_shapes=[
            pltpu.VMEM((count, width), jnp.bfloat16),
            pltpu.VMEM((4, depth, out_dim), jnp.bfloat16),
            pltpu.SemaphoreType.DMA((4,)),
        ],
        compiler_params=pltpu.CompilerParams(vmem_limit_bytes=24 << 20),
        cost_estimate=pl.CostEstimate(flops=3760000000, bytes_accessed=12000000, transcendentals=262144),
    )(expert.reshape(1).astype(jnp.int32), codes, *weights)


def interleave_kernel(core_ref, own_ref, other_ref, out_ref, staged, ordered, *, n_y, per_group):
    rows = own_ref.shape[0]
    in_block = rows // n_y
    n_group = in_block // per_group
    per_source = 2 * n_y * per_group
    tiles = own_ref.shape[1] // LANES

    def place(ref, core):
        for lane in range(tiles):
            staged[lane] = ref[:, lane * LANES : (lane + 1) * LANES].astype(jnp.float32)
        for lane in range(tiles):
            for y in range(n_y):
                for i in range(per_group):
                    to = pl.ds((2 * y + core) * per_group + i, n_group, stride=per_source)
                    ordered[lane, to, :] = staged[lane, pl.ds(y * in_block + i, n_group, stride=per_group), :]

    for core in range(2):

        @pl.when(core_ref[0] == core)
        def _():
            place(own_ref, core)
            place(other_ref, 1 - core)

    for lane in range(tiles):
        out_ref[:, lane * LANES : (lane + 1) * LANES] = ordered[lane].astype(out_ref.dtype)


def interleave(core, own, other, n_y, per_group):
    rows, width = own.shape
    return pl.pallas_call(
        functools.partial(interleave_kernel, n_y=n_y, per_group=per_group),
        out_shape=jax.ShapeDtypeStruct((2 * rows, width), own.dtype),
        in_specs=[pl.BlockSpec(memory_space=pltpu.SMEM)] + [pl.BlockSpec(memory_space=pltpu.VMEM)] * 2,
        out_specs=pl.BlockSpec(memory_space=pltpu.VMEM),
        scratch_shapes=[
            pltpu.VMEM((width // LANES, rows, LANES), jnp.float32),
            pltpu.VMEM((width // LANES, 2 * rows, LANES), jnp.float32),
        ],
        compiler_params=pltpu.CompilerParams(vmem_limit_bytes=8 << 20),
    )(core.reshape(1).astype(jnp.int32), own, other)


def shards(tokens, routes, route_gates, gate_weight, up_weight):
    n_group = lax.axis_size("group")
    n_local = lax.axis_size("local")
    n_y = n_local // 2
    width = tokens.shape[1]
    experts = n_group * EXP_MESH
    per_group = tokens.shape[0] // BLOCK
    local = lax.axis_index("local")
    core = local % 2
    my_expert = lax.axis_index("group") * EXP_MESH + local // (n_local // EXP_MESH)
    swap = [(2 * y + c, 2 * y + 1 - c) for y in range(n_y) for c in range(2)]
    same_core = [[2 * y + c for y in range(n_y)] for c in range(2)]

    packed = pack_rows(tokens, routes, route_gates, n_group, experts)
    received = lax.all_to_all(packed, "group", split_axis=0, concat_axis=0, tiled=True)
    other_gate = lax.ppermute(gate_weight, "local", swap)
    other_up = lax.ppermute(up_weight, "local", swap)
    received, other_gate, other_up = lax.optimization_barrier((received, other_gate, other_up))
    received = received.reshape(1, n_group * per_group, width + experts)
    gathered = lax.all_gather(received, "local", axis=0, axis_index_groups=same_core, tiled=True)
    gathered = gathered.reshape(-1, width + experts)

    for_other, own = multiply(my_expert, gathered, width, (other_gate[0], other_up[0], gate_weight[0], up_weight[0]))
    from_other = lax.ppermute(for_other, "local", swap)
    out = interleave(core, own, from_other, n_y, per_group)
    return out.reshape((1,) + out.shape)


def solution(mesh):
    placed = (
        P(("group", "local"), None),
        P(("group", "local"), None),
        P(("group", "local"), None),
        P(("group", "local"), None, None),
        P(("group", "local"), None, None),
    )
    return jax.shard_map(
        shards,
        mesh=mesh,
        in_specs=placed,
        out_specs=P(("group", "local"), None, None),
        check_vma=False,
    )
```

```python
import functools

import jax
import jax.numpy as jnp
from jax import lax
from jax.experimental import pallas as pl
from jax.experimental.pallas import tpu as pltpu
from jax.sharding import PartitionSpec as P

EXP_MESH = 4
BLOCK = 4
LANES = 128
CHUNKS = 4
GATE_ONE = 16000.0
CODE_MAX = 32000.0
EXP_BIAS = 200.0


def pack_kernel(tokens_ref, routes_ref, gates_ref, out_ref):
    count, width = tokens_ref.shape
    n_group, per_group, packed_width = out_ref.shape
    rows = n_group * per_group
    experts = packed_width - width
    tok = tokens_ref[...].astype(jnp.float32)
    largest = jnp.maximum(jnp.max(jnp.abs(tok), axis=1, keepdims=True), 1e-25)
    power = jnp.floor(jnp.log2(CODE_MAX / largest))
    codes = jnp.round(tok * jnp.exp2(power))
    routes = routes_ref[...]
    gate_codes = jnp.round(gates_ref[...] * GATE_ONE)
    expert = lax.broadcasted_iota(jnp.int32, (count, experts), 1)
    row = lax.broadcasted_iota(jnp.int32, (count, rows), 1)
    token = lax.broadcasted_iota(jnp.int32, (count, rows), 0)
    side = jnp.zeros((count, experts), jnp.float32)
    chosen = jnp.zeros((count, rows), jnp.float32)
    for k in range(routes.shape[1]):
        route = routes[:, k : k + 1]
        side = side + jnp.where(expert == route, gate_codes[:, k : k + 1], 0.0)
        chosen = jnp.where(route // EXP_MESH == row // per_group, 1.0, chosen)
    side = jnp.where(side > 0.0, side, -(power + EXP_BIAS))
    chosen = jnp.where(token // BLOCK == row % per_group, chosen, 0.0)
    chosen = chosen.T.astype(jnp.bfloat16)

    def send(values, first, size):
        high = jnp.floor(values * (1.0 / 256.0))
        low = values - 256.0 * high
        picked = jnp.dot(chosen, (256.0 * high).astype(jnp.bfloat16), preferred_element_type=jnp.float32)
        picked += jnp.dot(chosen, low.astype(jnp.bfloat16), preferred_element_type=jnp.float32)
        picked = picked.astype(jnp.int32).astype(jnp.int16)
        for group in range(n_group):
            out_ref[group, :, first : first + size] = picked[group * per_group : (group + 1) * per_group]

    send(codes, 0, width)
    send(side, width, experts)


def pack_rows(tokens, routes, route_gates, n_group, experts):
    count, width = tokens.shape
    return pl.pallas_call(
        pack_kernel,
        out_shape=jax.ShapeDtypeStruct((n_group, count // BLOCK, width + experts), jnp.int16),
        in_specs=[pl.BlockSpec(memory_space=pltpu.VMEM)] * 3,
        out_specs=pl.BlockSpec(memory_space=pltpu.VMEM),
    )(tokens, routes, route_gates)


def hidden_kernel(codes_ref, gate_ref, up_ref, out_ref, rows, held_up, arrived):
    width = rows.shape[1]
    copy = pltpu.make_async_copy(up_ref, held_up, arrived)
    copy.start()
    expert = lax.axis_index("group") * EXP_MESH + lax.axis_index("local") // (lax.axis_size("local") // EXP_MESH)
    rows[...] = codes_ref[:, :width].astype(jnp.float32).astype(jnp.bfloat16)
    side = codes_ref[:, width:].astype(jnp.float32)
    lane = lax.broadcasted_iota(jnp.int32, side.shape, 1)
    weight = jnp.sum(jnp.where(lane == expert, jnp.maximum(side, 0.0), 0.0), axis=1, keepdims=True)
    weight = weight * (1.0 / GATE_ONE)
    scale = jnp.exp2(jnp.min(side, axis=1, keepdims=True) + EXP_BIAS)
    pre_gate = jnp.dot(rows[...], gate_ref[...], preferred_element_type=jnp.float32) * scale
    copy.wait()
    pre_up = jnp.dot(rows[...], held_up[...], preferred_element_type=jnp.float32) * scale
    out_ref[...] = (pre_gate / (1.0 + jnp.exp(-pre_gate)) * pre_up * weight).astype(out_ref.dtype)


def hidden(codes, width, gate, up):
    count = codes.shape[0]
    out_dim = gate.shape[1]
    return pl.pallas_call(
        hidden_kernel,
        out_shape=jax.ShapeDtypeStruct((count, out_dim), jnp.bfloat16),
        in_specs=[pl.BlockSpec(memory_space=pltpu.VMEM)] * 2 + [pl.BlockSpec(memory_space=pl.ANY)],
        out_specs=pl.BlockSpec(memory_space=pltpu.VMEM),
        scratch_shapes=[
            pltpu.VMEM((count, width), jnp.bfloat16),
            pltpu.VMEM(up.shape, up.dtype),
            pltpu.SemaphoreType.DMA,
        ],
        compiler_params=pltpu.CompilerParams(vmem_limit_bytes=16 << 20),
        cost_estimate=pl.CostEstimate(flops=1880000000, bytes_accessed=8000000, transcendentals=131072),
    )(codes, gate, up)


def interleave_kernel(own_ref, other_ref, out_ref, staged, ordered, done, sent, *, n_y, per_group):
    in_block = own_ref.shape[0] // n_y
    n_group = in_block // per_group
    per_source = 2 * n_y * per_group
    tiles = own_ref.shape[1] // LANES
    my_core = lax.axis_index("local") % 2
    for lane in range(tiles):
        cols = slice(lane * LANES, (lane + 1) * LANES)
        staged[lane, 0] = own_ref[:, cols].astype(jnp.float32)
        staged[lane, 1] = other_ref[:, cols].astype(jnp.float32)
    groups = n_group // CHUNKS
    copies = []
    for chunk in range(CHUNKS):
        for core in range(2):

            @pl.when(my_core == core)
            def _():
                for lane in range(tiles):
                    for y in range(n_y):
                        for i in range(per_group):
                            start = y * in_block + chunk * groups * per_group + i
                            origin = pl.ds(start, groups, stride=per_group)
                            for source in range(2):
                                place = core if source == 0 else 1 - core
                                target = chunk * groups * per_source + (2 * y + place) * per_group + i
                                ordered[lane, pl.ds(target, groups, stride=per_source), :] = staged[
                                    lane, source, origin, :
                                ]

        rows = slice(chunk * groups * per_source, (chunk + 1) * groups * per_source)
        for lane in range(tiles):
            done[rows, lane * LANES : (lane + 1) * LANES] = ordered[lane, rows].astype(done.dtype)
        copy = pltpu.make_async_copy(done.at[rows], out_ref.at[rows], sent.at[chunk])
        copy.start()
        copies.append(copy)
    for copy in copies:
        copy.wait()


def interleave(own, other, n_y, per_group):
    rows, width = own.shape
    tiles = width // LANES
    return pl.pallas_call(
        functools.partial(interleave_kernel, n_y=n_y, per_group=per_group),
        out_shape=jax.ShapeDtypeStruct((2 * rows, width), own.dtype),
        in_specs=[pl.BlockSpec(memory_space=pltpu.VMEM)] * 2,
        out_specs=pl.BlockSpec(memory_space=pl.ANY),
        scratch_shapes=[
            pltpu.VMEM((tiles, 2, rows, LANES), jnp.float32),
            pltpu.VMEM((tiles, 2 * rows, LANES), jnp.float32),
            pltpu.VMEM((2 * rows, width), own.dtype),
            pltpu.SemaphoreType.DMA((CHUNKS,)),
        ],
        compiler_params=pltpu.CompilerParams(vmem_limit_bytes=8 << 20),
        cost_estimate=pl.CostEstimate(flops=0, bytes_accessed=1000000, transcendentals=0),
    )(own, other)


def shards(tokens, routes, route_gates, gate_weight, up_weight):
    n_group = lax.axis_size("group")
    n_local = lax.axis_size("local")
    n_y = n_local // 2
    width = tokens.shape[1]
    experts = n_group * EXP_MESH
    per_group = tokens.shape[0] // BLOCK
    swap = [(2 * y + c, 2 * y + 1 - c) for y in range(n_y) for c in range(2)]
    same_core = [[2 * y + c for y in range(n_y)] for c in range(2)]

    packed = pack_rows(tokens, routes, route_gates, n_group, experts)
    received = lax.all_to_all(packed, "group", split_axis=0, concat_axis=0, tiled=True)
    other_gate = lax.ppermute(gate_weight, "local", swap)
    other_up = lax.ppermute(up_weight, "local", swap)
    received, other_gate, other_up = lax.optimization_barrier((received, other_gate, other_up))
    received = received.reshape(1, n_group * per_group, width + experts)
    gathered = lax.all_gather(received, "local", axis=0, axis_index_groups=same_core, tiled=True)
    gathered = gathered.reshape(-1, width + experts)

    for_other = hidden(gathered, width, other_gate[0], other_up[0])
    from_other = lax.ppermute(for_other, "local", swap)
    own = hidden(gathered, width, gate_weight[0], up_weight[0])
    out = interleave(own, from_other, n_y, per_group)
    return out.reshape((1,) + out.shape)


def solution(mesh):
    placed = (
        P(("group", "local"), None),
        P(("group", "local"), None),
        P(("group", "local"), None),
        P(("group", "local"), None, None),
        P(("group", "local"), None, None),
    )
    return jax.shard_map(
        shards,
        mesh=mesh,
        in_specs=placed,
        out_specs=P(("group", "local"), None, None),
        check_vma=False,
    )
```

```python
import functools

import jax
import jax.numpy as jnp
from jax import lax
from jax.experimental import pallas as pl
from jax.experimental.pallas import tpu as pltpu
from jax.sharding import PartitionSpec as P

EXP_MESH = 4
BLOCK = 4
LANES = 128
CHUNKS = 4
GATE_ONE = 16000.0
CODE_MAX = 32000.0
EXP_BIAS = 200.0


def pack_kernel(tokens_ref, routes_ref, gates_ref, out_ref):
    count, width = tokens_ref.shape
    n_group, per_group, packed_width = out_ref.shape
    rows = n_group * per_group
    experts = packed_width - width
    tok = tokens_ref[...].astype(jnp.float32)
    largest = jnp.maximum(jnp.max(jnp.abs(tok), axis=1, keepdims=True), 1e-25)
    power = jnp.floor(jnp.log2(CODE_MAX / largest))
    codes = jnp.round(tok * jnp.exp2(power))
    routes = routes_ref[...]
    gate_codes = jnp.round(gates_ref[...] * GATE_ONE)
    expert = lax.broadcasted_iota(jnp.int32, (count, experts), 1)
    row = lax.broadcasted_iota(jnp.int32, (count, rows), 1)
    token = lax.broadcasted_iota(jnp.int32, (count, rows), 0)
    side = jnp.zeros((count, experts), jnp.float32)
    chosen = jnp.zeros((count, rows), jnp.float32)
    for k in range(routes.shape[1]):
        route = routes[:, k : k + 1]
        side = side + jnp.where(expert == route, gate_codes[:, k : k + 1], 0.0)
        chosen = jnp.where(route // EXP_MESH == row // per_group, 1.0, chosen)
    side = jnp.where(side > 0.0, side, -(power + EXP_BIAS))
    chosen = jnp.where(token // BLOCK == row % per_group, chosen, 0.0)
    chosen = chosen.T.astype(jnp.bfloat16)

    def send(values, first, size):
        high = jnp.floor(values * (1.0 / 256.0))
        low = values - 256.0 * high
        picked = jnp.dot(chosen, (256.0 * high).astype(jnp.bfloat16), preferred_element_type=jnp.float32)
        picked += jnp.dot(chosen, low.astype(jnp.bfloat16), preferred_element_type=jnp.float32)
        picked = picked.astype(jnp.int32).astype(jnp.int16)
        for group in range(n_group):
            out_ref[group, :, first : first + size] = picked[group * per_group : (group + 1) * per_group]

    send(codes, 0, width)
    send(side, width, experts)


def pack_rows(tokens, routes, route_gates, n_group, experts):
    count, width = tokens.shape
    return pl.pallas_call(
        pack_kernel,
        out_shape=jax.ShapeDtypeStruct((n_group, count // BLOCK, width + experts), jnp.int16),
        in_specs=[pl.BlockSpec(memory_space=pltpu.VMEM)] * 3,
        out_specs=pl.BlockSpec(memory_space=pltpu.VMEM),
    )(tokens, routes, route_gates)


def hidden_kernel(codes_ref, gate_ref, up_ref, gate_of_other_ref, up_of_other_ref, own_ref, other_ref, rows, held, arrived):
    width = rows.shape[1]
    copy = pltpu.make_async_copy(up_of_other_ref, held, arrived)
    copy.start()
    expert = lax.axis_index("group") * EXP_MESH + lax.axis_index("local") // (lax.axis_size("local") // EXP_MESH)
    rows[...] = codes_ref[:, :width].astype(jnp.float32).astype(jnp.bfloat16)
    side = codes_ref[:, width:].astype(jnp.float32)
    lane = lax.broadcasted_iota(jnp.int32, side.shape, 1)
    weight = jnp.sum(jnp.where(lane == expert, jnp.maximum(side, 0.0), 0.0), axis=1, keepdims=True)
    weight = weight * (1.0 / GATE_ONE)
    scale = jnp.exp2(jnp.min(side, axis=1, keepdims=True) + EXP_BIAS)

    def multiply(gate, up, out_ref):
        pre_gate = jnp.dot(rows[...], gate[...], preferred_element_type=jnp.float32) * scale
        pre_up = jnp.dot(rows[...], up[...], preferred_element_type=jnp.float32) * scale
        out_ref[...] = (pre_gate / (1.0 + jnp.exp(-pre_gate)) * pre_up * weight).astype(out_ref.dtype)

    multiply(gate_ref, up_ref, own_ref)
    copy.wait()
    multiply(gate_of_other_ref, held, other_ref)


def hidden(codes, width, weights):
    count = codes.shape[0]
    shape = weights[0].shape
    return pl.pallas_call(
        hidden_kernel,
        out_shape=[jax.ShapeDtypeStruct((count, shape[1]), jnp.bfloat16)] * 2,
        in_specs=[pl.BlockSpec(memory_space=pltpu.VMEM)] * 4 + [pl.BlockSpec(memory_space=pl.ANY)],
        out_specs=[pl.BlockSpec(memory_space=pltpu.VMEM)] * 2,
        scratch_shapes=[
            pltpu.VMEM((count, width), jnp.bfloat16),
            pltpu.VMEM(shape, jnp.bfloat16),
            pltpu.SemaphoreType.DMA,
        ],
        compiler_params=pltpu.CompilerParams(vmem_limit_bytes=16 << 20),
        cost_estimate=pl.CostEstimate(flops=3760000000, bytes_accessed=12000000, transcendentals=262144),
    )(codes, *weights)


def interleave_kernel(own_ref, other_ref, out_ref, staged, ordered, done, sent, *, n_y, per_group):
    in_block = own_ref.shape[0] // n_y
    n_group = in_block // per_group
    per_source = 2 * n_y * per_group
    tiles = own_ref.shape[1] // LANES
    my_core = lax.axis_index("local") % 2
    for lane in range(tiles):
        cols = slice(lane * LANES, (lane + 1) * LANES)
        staged[lane, 0] = own_ref[:, cols].astype(jnp.float32)
        staged[lane, 1] = other_ref[:, cols].astype(jnp.float32)
    groups = n_group // CHUNKS
    copies = []
    for chunk in range(CHUNKS):
        for core in range(2):

            @pl.when(my_core == core)
            def _():
                for lane in range(tiles):
                    for y in range(n_y):
                        for i in range(per_group):
                            start = y * in_block + chunk * groups * per_group + i
                            origin = pl.ds(start, groups, stride=per_group)
                            for source in range(2):
                                place = core if source == 0 else 1 - core
                                target = chunk * groups * per_source + (2 * y + place) * per_group + i
                                ordered[lane, pl.ds(target, groups, stride=per_source), :] = staged[
                                    lane, source, origin, :
                                ]

        rows = slice(chunk * groups * per_source, (chunk + 1) * groups * per_source)
        for lane in range(tiles):
            done[rows, lane * LANES : (lane + 1) * LANES] = ordered[lane, rows].astype(done.dtype)
        copy = pltpu.make_async_copy(done.at[rows], out_ref.at[rows], sent.at[chunk])
        copy.start()
        copies.append(copy)
    for copy in copies:
        copy.wait()


def interleave(own, other, n_y, per_group):
    rows, width = own.shape
    tiles = width // LANES
    return pl.pallas_call(
        functools.partial(interleave_kernel, n_y=n_y, per_group=per_group),
        out_shape=jax.ShapeDtypeStruct((2 * rows, width), own.dtype),
        in_specs=[pl.BlockSpec(memory_space=pltpu.VMEM)] * 2,
        out_specs=pl.BlockSpec(memory_space=pl.ANY),
        scratch_shapes=[
            pltpu.VMEM((tiles, 2, rows, LANES), jnp.float32),
            pltpu.VMEM((tiles, 2 * rows, LANES), jnp.float32),
            pltpu.VMEM((2 * rows, width), own.dtype),
            pltpu.SemaphoreType.DMA((CHUNKS,)),
        ],
        compiler_params=pltpu.CompilerParams(vmem_limit_bytes=8 << 20),
        cost_estimate=pl.CostEstimate(flops=0, bytes_accessed=1000000, transcendentals=0),
    )(own, other)


def shards(tokens, routes, route_gates, gate_weight, up_weight):
    n_group = lax.axis_size("group")
    n_local = lax.axis_size("local")
    n_y = n_local // 2
    width = tokens.shape[1]
    experts = n_group * EXP_MESH
    per_group = tokens.shape[0] // BLOCK
    swap = [(2 * y + c, 2 * y + 1 - c) for y in range(n_y) for c in range(2)]
    same_core = [[2 * y + c for y in range(n_y)] for c in range(2)]

    packed = pack_rows(tokens, routes, route_gates, n_group, experts)
    received = lax.all_to_all(packed, "group", split_axis=0, concat_axis=0, tiled=True)
    other_gate = lax.ppermute(gate_weight, "local", swap)
    other_up = lax.ppermute(up_weight, "local", swap)
    received, other_gate, other_up = lax.optimization_barrier((received, other_gate, other_up))
    received = received.reshape(1, n_group * per_group, width + experts)
    gathered = lax.all_gather(received, "local", axis=0, axis_index_groups=same_core, tiled=True)
    gathered = gathered.reshape(-1, width + experts)

    own, for_other = hidden(gathered, width, (gate_weight[0], up_weight[0], other_gate[0], other_up[0]))
    from_other = lax.ppermute(for_other, "local", swap)
    out = interleave(own, from_other, n_y, per_group)
    return out.reshape((1,) + out.shape)


def solution(mesh):
    placed = (
        P(("group", "local"), None),
        P(("group", "local"), None),
        P(("group", "local"), None),
        P(("group", "local"), None, None),
        P(("group", "local"), None, None),
    )
    return jax.shard_map(
        shards,
        mesh=mesh,
        in_specs=placed,
        out_specs=P(("group", "local"), None, None),
        check_vma=False,
    )
```

```python
import functools

import jax
import jax.numpy as jnp
from jax import lax
from jax.experimental import pallas as pl
from jax.experimental.pallas import tpu as pltpu
from jax.sharding import PartitionSpec as P

EXP_MESH = 4
BLOCK = 4
LANES = 128
CHUNKS = 4
GATE_ONE = 16000.0
CODE_MAX = 32000.0
EXP_BIAS = 200.0


def pack_kernel(tokens_ref, routes_ref, gates_ref, out_ref, staged, sent):
    count, width = tokens_ref.shape
    n_group, per_group, packed_width = out_ref.shape
    rows = n_group * per_group
    experts = packed_width - width
    tok = tokens_ref[...].astype(jnp.float32)
    largest = jnp.maximum(jnp.max(jnp.abs(tok), axis=1, keepdims=True), 1e-25)
    power = jnp.floor(jnp.log2(CODE_MAX / largest))
    codes = jnp.round(tok * jnp.exp2(power))
    routes = routes_ref[...]
    gate_codes = jnp.round(gates_ref[...] * GATE_ONE)
    expert = lax.broadcasted_iota(jnp.int32, (count, experts), 1)
    row = lax.broadcasted_iota(jnp.int32, (count, rows), 1)
    token = lax.broadcasted_iota(jnp.int32, (count, rows), 0)
    side = jnp.zeros((count, experts), jnp.float32)
    chosen = jnp.zeros((count, rows), jnp.float32)
    for k in range(routes.shape[1]):
        route = routes[:, k : k + 1]
        side = side + jnp.where(expert == route, gate_codes[:, k : k + 1], 0.0)
        chosen = jnp.where(route // EXP_MESH == row // per_group, 1.0, chosen)
    side = jnp.where(side > 0.0, side, -(power + EXP_BIAS))
    chosen = jnp.where(token // BLOCK == row % per_group, chosen, 0.0)
    chosen = chosen.T.astype(jnp.bfloat16)

    copies = []

    def send(values, first, size):
        high = jnp.floor(values * (1.0 / 256.0))
        low = values - 256.0 * high
        picked = jnp.dot(chosen, (256.0 * high).astype(jnp.bfloat16), preferred_element_type=jnp.float32)
        picked += jnp.dot(chosen, low.astype(jnp.bfloat16), preferred_element_type=jnp.float32)
        picked = picked.astype(jnp.int32).astype(jnp.int16)
        for group in range(n_group):
            staged[group, :, first : first + size] = picked[group * per_group : (group + 1) * per_group]
        cols = pl.ds(first, size)
        copy = pltpu.make_async_copy(staged.at[:, :, cols], out_ref.at[:, :, cols], sent.at[len(copies)])
        copy.start()
        copies.append(copy)

    send(side, width, experts)
    piece = width // CHUNKS
    for chunk in range(CHUNKS):
        send(codes[:, chunk * piece : (chunk + 1) * piece], chunk * piece, piece)
    for copy in copies:
        copy.wait()


def pack_rows(tokens, routes, route_gates, n_group, experts):
    count, width = tokens.shape
    return pl.pallas_call(
        pack_kernel,
        out_shape=jax.ShapeDtypeStruct((n_group, count // BLOCK, width + experts), jnp.int16),
        in_specs=[pl.BlockSpec(memory_space=pltpu.VMEM)] * 3,
        out_specs=pl.BlockSpec(memory_space=pl.ANY),
        scratch_shapes=[
            pltpu.VMEM((n_group, count // BLOCK, width + experts), jnp.int16),
            pltpu.SemaphoreType.DMA((CHUNKS + 1,)),
        ],
    )(tokens, routes, route_gates)


def scale_and_weight(side_ref):
    expert = lax.axis_index("group") * EXP_MESH + lax.axis_index("local") // (lax.axis_size("local") // EXP_MESH)
    side = side_ref[...].astype(jnp.float32)
    lane = lax.broadcasted_iota(jnp.int32, side.shape, 1)
    weight = jnp.sum(jnp.where(lane == expert, jnp.maximum(side, 0.0), 0.0), axis=1, keepdims=True)
    return jnp.exp2(jnp.min(side, axis=1, keepdims=True) + EXP_BIAS), weight * (1.0 / GATE_ONE)


def gated(pre_gate, pre_up, scale, weight, out_ref):
    pre_gate = pre_gate * scale
    out_ref[...] = (pre_gate / (1.0 + jnp.exp(-pre_gate)) * (pre_up * scale) * weight).astype(out_ref.dtype)


def other_kernel(codes_ref, gate_ref, up_hbm, gate_later, up_later, out_ref, rows, held, arrived):
    width = rows.shape[1]
    copy = pltpu.make_async_copy(up_hbm, held, arrived)
    copy.start()
    rows[...] = codes_ref[:, :width].astype(jnp.float32).astype(jnp.bfloat16)
    scale, weight = scale_and_weight(codes_ref.at[:, width:])
    pre_gate = jnp.dot(rows[...], gate_ref[...], preferred_element_type=jnp.float32)
    copy.wait()
    pre_up = jnp.dot(rows[...], held[...], preferred_element_type=jnp.float32)
    gated(pre_gate, pre_up, scale, weight, out_ref)


def own_kernel(codes_ref, rows, gate_ref, up_ref, out_ref):
    scale, weight = scale_and_weight(codes_ref.at[:, rows.shape[1] :])
    pre_gate = jnp.dot(rows[...], gate_ref[...], preferred_element_type=jnp.float32)
    pre_up = jnp.dot(rows[...], up_ref[...], preferred_element_type=jnp.float32)
    gated(pre_gate, pre_up, scale, weight, out_ref)


def hidden_of_other(codes, width, gate, up, gate_later, up_later):
    count = codes.shape[0]
    in_vmem = pl.BlockSpec(memory_space=pltpu.VMEM)
    return pl.pallas_call(
        other_kernel,
        out_shape=[
            jax.ShapeDtypeStruct((count, gate.shape[1]), jnp.bfloat16),
            jax.ShapeDtypeStruct((count, width), jnp.bfloat16),
        ],
        in_specs=[in_vmem, in_vmem, pl.BlockSpec(memory_space=pl.ANY), in_vmem, in_vmem],
        out_specs=[in_vmem, in_vmem],
        scratch_shapes=[pltpu.VMEM(up.shape, up.dtype), pltpu.SemaphoreType.DMA],
        compiler_params=pltpu.CompilerParams(vmem_limit_bytes=16 << 20),
        cost_estimate=pl.CostEstimate(flops=1880000000, bytes_accessed=12000000, transcendentals=131072),
    )(codes, gate, up, gate_later, up_later)


def hidden_of_own(codes, rows, gate, up):
    in_vmem = pl.BlockSpec(memory_space=pltpu.VMEM)
    return pl.pallas_call(
        own_kernel,
        out_shape=jax.ShapeDtypeStruct((rows.shape[0], gate.shape[1]), jnp.bfloat16),
        in_specs=[in_vmem] * 4,
        out_specs=in_vmem,
        compiler_params=pltpu.CompilerParams(vmem_limit_bytes=16 << 20),
        cost_estimate=pl.CostEstimate(flops=1880000000, bytes_accessed=12000000, transcendentals=131072),
    )(codes, rows, gate, up)


def interleave_kernel(own_ref, other_ref, out_ref, staged, ordered, done, sent, *, n_y, per_group):
    in_block = own_ref.shape[0] // n_y
    n_group = in_block // per_group
    per_source = 2 * n_y * per_group
    tiles = own_ref.shape[1] // LANES
    my_core = lax.axis_index("local") % 2
    for lane in range(tiles):
        cols = slice(lane * LANES, (lane + 1) * LANES)
        staged[lane, 0] = own_ref[:, cols].astype(jnp.float32)
        staged[lane, 1] = other_ref[:, cols].astype(jnp.float32)
    groups = n_group // CHUNKS
    copies = []
    for chunk in range(CHUNKS):
        for core in range(2):

            @pl.when(my_core == core)
            def _():
                for lane in range(tiles):
                    for y in range(n_y):
                        for i in range(per_group):
                            start = y * in_block + chunk * groups * per_group + i
                            origin = pl.ds(start, groups, stride=per_group)
                            for source in range(2):
                                place = core if source == 0 else 1 - core
                                target = chunk * groups * per_source + (2 * y + place) * per_group + i
                                ordered[lane, pl.ds(target, groups, stride=per_source), :] = staged[
                                    lane, source, origin, :
                                ]

        rows = slice(chunk * groups * per_source, (chunk + 1) * groups * per_source)
        for lane in range(tiles):
            done[rows, lane * LANES : (lane + 1) * LANES] = ordered[lane, rows].astype(done.dtype)
        copy = pltpu.make_async_copy(done.at[rows], out_ref.at[rows], sent.at[chunk])
        copy.start()
        copies.append(copy)
    for copy in copies:
        copy.wait()


def interleave(own, other, n_y, per_group):
    rows, width = own.shape
    tiles = width // LANES
    return pl.pallas_call(
        functools.partial(interleave_kernel, n_y=n_y, per_group=per_group),
        out_shape=jax.ShapeDtypeStruct((2 * rows, width), own.dtype),
        in_specs=[pl.BlockSpec(memory_space=pltpu.VMEM)] * 2,
        out_specs=pl.BlockSpec(memory_space=pl.ANY),
        scratch_shapes=[
            pltpu.VMEM((tiles, 2, rows, LANES), jnp.float32),
            pltpu.VMEM((tiles, 2 * rows, LANES), jnp.float32),
            pltpu.VMEM((2 * rows, width), own.dtype),
            pltpu.SemaphoreType.DMA((CHUNKS,)),
        ],
        compiler_params=pltpu.CompilerParams(vmem_limit_bytes=8 << 20),
        cost_estimate=pl.CostEstimate(flops=0, bytes_accessed=1000000, transcendentals=0),
    )(own, other)


def shards(tokens, routes, route_gates, gate_weight, up_weight):
    n_group = lax.axis_size("group")
    n_local = lax.axis_size("local")
    n_y = n_local // 2
    width = tokens.shape[1]
    experts = n_group * EXP_MESH
    per_group = tokens.shape[0] // BLOCK
    swap = [(2 * y + c, 2 * y + 1 - c) for y in range(n_y) for c in range(2)]
    same_core = [[2 * y + c for y in range(n_y)] for c in range(2)]

    packed = pack_rows(tokens, routes, route_gates, n_group, experts)
    received = lax.all_to_all(packed, "group", split_axis=0, concat_axis=0, tiled=True)
    other_gate = lax.ppermute(gate_weight, "local", swap)
    other_up = lax.ppermute(up_weight, "local", swap)
    received, other_gate, other_up = lax.optimization_barrier((received, other_gate, other_up))
    received = received.reshape(1, n_group * per_group, width + experts)
    gathered = lax.all_gather(received, "local", axis=0, axis_index_groups=same_core, tiled=True)
    gathered = gathered.reshape(-1, width + experts)

    for_other, rows = hidden_of_other(
        gathered, width, other_gate[0], other_up[0], gate_weight[0], up_weight[0]
    )
    from_other = lax.ppermute(for_other, "local", swap)
    own = hidden_of_own(gathered, rows, gate_weight[0], up_weight[0])
    out = interleave(own, from_other, n_y, per_group)
    return out.reshape((1,) + out.shape)


def solution(mesh):
    placed = (
        P(("group", "local"), None),
        P(("group", "local"), None),
        P(("group", "local"), None),
        P(("group", "local"), None, None),
        P(("group", "local"), None, None),
    )
    return jax.shard_map(
        shards,
        mesh=mesh,
        in_specs=placed,
        out_specs=P(("group", "local"), None, None),
        check_vma=False,
    )
```

```python
import functools

import jax
import jax.numpy as jnp
from jax import lax
from jax.experimental import pallas as pl
from jax.experimental.pallas import tpu as pltpu
from jax.sharding import PartitionSpec as P

EXP_MESH = 4
BLOCK = 4
CHUNKS = 4
GATE_ONE = 16000.0
CODE_MAX = 32000.0
EXP_BIAS = 200.0


def pack_kernel(tokens_ref, routes_ref, gates_ref, out_ref, staged, sent):
    count, width = tokens_ref.shape
    n_group, per_group, packed_width = out_ref.shape
    rows = n_group * per_group
    experts = packed_width - width
    tok = tokens_ref[...].astype(jnp.float32)
    largest = jnp.maximum(jnp.max(jnp.abs(tok), axis=1, keepdims=True), 1e-25)
    power = jnp.floor(jnp.log2(CODE_MAX / largest))
    codes = jnp.round(tok * jnp.exp2(power))
    routes = routes_ref[...]
    gate_codes = jnp.round(gates_ref[...] * GATE_ONE)
    expert = lax.broadcasted_iota(jnp.int32, (count, experts), 1)
    row = lax.broadcasted_iota(jnp.int32, (count, rows), 1)
    token = lax.broadcasted_iota(jnp.int32, (count, rows), 0)
    side = jnp.zeros((count, experts), jnp.float32)
    chosen = jnp.zeros((count, rows), jnp.float32)
    for k in range(routes.shape[1]):
        route = routes[:, k : k + 1]
        side = side + jnp.where(expert == route, gate_codes[:, k : k + 1], 0.0)
        chosen = jnp.where(route // EXP_MESH == row // per_group, 1.0, chosen)
    side = jnp.where(side > 0.0, side, -(power + EXP_BIAS))
    chosen = jnp.where(token // BLOCK == row % per_group, chosen, 0.0)
    chosen = chosen.T.astype(jnp.bfloat16)

    copies = []

    def send(values, first, size):
        high = jnp.floor(values * (1.0 / 256.0))
        low = values - 256.0 * high
        picked = jnp.dot(chosen, (256.0 * high).astype(jnp.bfloat16), preferred_element_type=jnp.float32)
        picked += jnp.dot(chosen, low.astype(jnp.bfloat16), preferred_element_type=jnp.float32)
        picked = picked.astype(jnp.int32).astype(jnp.int16)
        for group in range(n_group):
            staged[group, :, first : first + size] = picked[group * per_group : (group + 1) * per_group]
        cols = pl.ds(first, size)
        copy = pltpu.make_async_copy(staged.at[:, :, cols], out_ref.at[:, :, cols], sent.at[len(copies)])
        copy.start()
        copies.append(copy)

    send(side, width, experts)
    piece = width // CHUNKS
    for chunk in range(CHUNKS):
        send(codes[:, chunk * piece : (chunk + 1) * piece], chunk * piece, piece)
    for copy in copies:
        copy.wait()


def pack_rows(tokens, routes, route_gates, n_group, experts):
    count, width = tokens.shape
    return pl.pallas_call(
        pack_kernel,
        out_shape=jax.ShapeDtypeStruct((n_group, count // BLOCK, width + experts), jnp.int16),
        in_specs=[pl.BlockSpec(memory_space=pltpu.VMEM)] * 3,
        out_specs=pl.BlockSpec(memory_space=pl.ANY),
        scratch_shapes=[
            pltpu.VMEM((n_group, count // BLOCK, width + experts), jnp.int16),
            pltpu.SemaphoreType.DMA((CHUNKS + 1,)),
        ],
    )(tokens, routes, route_gates)


def scale_and_weight(side_ref):
    expert = lax.axis_index("group") * EXP_MESH + lax.axis_index("local") // (lax.axis_size("local") // EXP_MESH)
    side = side_ref[...].astype(jnp.float32)
    lane = lax.broadcasted_iota(jnp.int32, side.shape, 1)
    weight = jnp.sum(jnp.where(lane == expert, jnp.maximum(side, 0.0), 0.0), axis=1, keepdims=True)
    return jnp.exp2(jnp.min(side, axis=1, keepdims=True) + EXP_BIAS), weight * (1.0 / GATE_ONE)


def gated(pre_gate, pre_up, scale, weight):
    pre_gate = pre_gate * scale
    return (pre_gate / (1.0 + jnp.exp(-pre_gate)) * (pre_up * scale) * weight).astype(jnp.bfloat16)


def placement(core, n_y, per_group, rows):
    in_block = rows // n_y
    per_source = 2 * n_y * per_group
    at = lax.broadcasted_iota(jnp.int32, (2 * rows, 1), 0)
    pair = at // per_group
    source = (at % per_source) // (2 * per_group) * in_block + at // per_source * per_group + at % per_group
    source = jnp.where(pair % 2 == core, source, -1)
    return (lax.broadcasted_iota(jnp.int32, (2 * rows, rows), 1) == source).astype(jnp.float32).astype(jnp.bfloat16)


def other_kernel(codes_ref, gate_of_own, gate_ref, up_hbm, up_later, out_ref, own_gate_ref, rows, held, arrived):
    width = rows.shape[1]
    copy = pltpu.make_async_copy(up_hbm, held, arrived)
    copy.start()
    rows[...] = codes_ref[:, :width].astype(jnp.float32).astype(jnp.bfloat16)
    scale, weight = scale_and_weight(codes_ref.at[:, width:])
    own_gate_ref[...] = jnp.dot(rows[...], gate_of_own[...], preferred_element_type=jnp.float32)
    pre_gate = jnp.dot(rows[...], gate_ref[...], preferred_element_type=jnp.float32)
    copy.wait()
    pre_up = jnp.dot(rows[...], held[...], preferred_element_type=jnp.float32)
    out_ref[...] = gated(pre_gate, pre_up, scale, weight)


def own_kernel(codes_ref, rows, gate_of_own, up_ref, placed_ref, place_ref, *, n_y, per_group):
    core = lax.axis_index("local") % 2
    scale, weight = scale_and_weight(codes_ref.at[:, rows.shape[1] :])
    pre_up = jnp.dot(rows[...], up_ref[...], preferred_element_type=jnp.float32)
    own = gated(gate_of_own[...], pre_up, scale, weight)
    place = placement(core, n_y, per_group, rows.shape[0])
    placed_ref[...] = jnp.dot(place, own, preferred_element_type=jnp.float32).astype(placed_ref.dtype)
    place_ref[...] = placement(1 - core, n_y, per_group, rows.shape[0])


def join_kernel(placed_ref, place_ref, other_ref, out_hbm, joined, sent):
    piece = joined.shape[0] // CHUNKS
    copies = []
    for chunk in range(CHUNKS):
        rows = slice(chunk * piece, (chunk + 1) * piece)
        other = jnp.dot(place_ref[rows], other_ref[...], preferred_element_type=jnp.float32)
        joined[rows] = (placed_ref[rows].astype(jnp.float32) + other).astype(joined.dtype)
        copy = pltpu.make_async_copy(joined.at[rows], out_hbm.at[rows], sent.at[chunk])
        copy.start()
        copies.append(copy)
    for copy in copies:
        copy.wait()


def hidden_of_other(codes, width, gate_of_own, gate, up, up_later):
    count = codes.shape[0]
    out_dim = gate.shape[1]
    in_vmem = pl.BlockSpec(memory_space=pltpu.VMEM)
    return pl.pallas_call(
        other_kernel,
        out_shape=[
            jax.ShapeDtypeStruct((count, out_dim), jnp.bfloat16),
            jax.ShapeDtypeStruct((count, out_dim), jnp.float32),
            jax.ShapeDtypeStruct((count, width), jnp.bfloat16),
        ],
        in_specs=[in_vmem, in_vmem, in_vmem, pl.BlockSpec(memory_space=pl.ANY), in_vmem],
        out_specs=[in_vmem] * 3,
        scratch_shapes=[pltpu.VMEM(up.shape, up.dtype), pltpu.SemaphoreType.DMA],
        compiler_params=pltpu.CompilerParams(vmem_limit_bytes=16 << 20),
        cost_estimate=pl.CostEstimate(flops=2820000000, bytes_accessed=12000000, transcendentals=131072),
    )(codes, gate_of_own, gate, up, up_later)


def hidden_of_own(codes, rows, gate_of_own, up, n_y, per_group):
    count = rows.shape[0]
    in_vmem = pl.BlockSpec(memory_space=pltpu.VMEM)
    return pl.pallas_call(
        functools.partial(own_kernel, n_y=n_y, per_group=per_group),
        out_shape=[
            jax.ShapeDtypeStruct((2 * count, up.shape[1]), jnp.bfloat16),
            jax.ShapeDtypeStruct((2 * count, count), jnp.bfloat16),
        ],
        in_specs=[in_vmem] * 4,
        out_specs=[in_vmem] * 2,
        compiler_params=pltpu.CompilerParams(vmem_limit_bytes=16 << 20),
        cost_estimate=pl.CostEstimate(flops=940000000, bytes_accessed=12000000, transcendentals=131072),
    )(codes, rows, gate_of_own, up)


def join(placed, place, other):
    in_vmem = pl.BlockSpec(memory_space=pltpu.VMEM)
    return pl.pallas_call(
        join_kernel,
        out_shape=jax.ShapeDtypeStruct(placed.shape, placed.dtype),
        in_specs=[in_vmem] * 3,
        out_specs=pl.BlockSpec(memory_space=pl.ANY),
        scratch_shapes=[pltpu.VMEM(placed.shape, placed.dtype), pltpu.SemaphoreType.DMA((CHUNKS,))],
        compiler_params=pltpu.CompilerParams(vmem_limit_bytes=8 << 20),
        cost_estimate=pl.CostEstimate(flops=270000000, bytes_accessed=2000000, transcendentals=0),
    )(placed, place, other)


def shards(tokens, routes, route_gates, gate_weight, up_weight):
    n_group = lax.axis_size("group")
    n_local = lax.axis_size("local")
    n_y = n_local // 2
    width = tokens.shape[1]
    experts = n_group * EXP_MESH
    per_group = tokens.shape[0] // BLOCK
    swap = [(2 * y + c, 2 * y + 1 - c) for y in range(n_y) for c in range(2)]
    same_core = [[2 * y + c for y in range(n_y)] for c in range(2)]

    packed = pack_rows(tokens, routes, route_gates, n_group, experts)
    received = lax.all_to_all(packed, "group", split_axis=0, concat_axis=0, tiled=True)
    other_gate = lax.ppermute(gate_weight, "local", swap)
    other_up = lax.ppermute(up_weight, "local", swap)
    received, other_gate, other_up = lax.optimization_barrier((received, other_gate, other_up))
    received = received.reshape(1, n_group * per_group, width + experts)
    gathered = lax.all_gather(received, "local", axis=0, axis_index_groups=same_core, tiled=True)
    gathered = gathered.reshape(-1, width + experts)

    for_other, gate_of_own, rows = hidden_of_other(
        gathered, width, gate_weight[0], other_gate[0], other_up[0], up_weight[0]
    )
    from_other = lax.ppermute(for_other, "local", swap)
    placed, place = hidden_of_own(gathered, rows, gate_of_own, up_weight[0], n_y, per_group)
    out = join(placed, place, from_other)
    return out.reshape((1,) + out.shape)


def solution(mesh):
    placed = (
        P(("group", "local"), None),
        P(("group", "local"), None),
        P(("group", "local"), None),
        P(("group", "local"), None, None),
        P(("group", "local"), None, None),
    )
    return jax.shard_map(
        shards,
        mesh=mesh,
        in_specs=placed,
        out_specs=P(("group", "local"), None, None),
        check_vma=False,
    )
```

```python
import functools

import jax
import jax.numpy as jnp
from jax import lax
from jax.experimental import pallas as pl
from jax.experimental.pallas import tpu as pltpu
from jax.sharding import PartitionSpec as P

EXP_MESH = 4
BLOCK = 4
LANES = 128
CHUNKS = 4
GATE_ONE = 16000.0
CODE_MAX = 32000.0
EXP_BIAS = 200.0


def pack_kernel(tokens_ref, routes_ref, gates_ref, out_ref, staged, sent):
    count, width = tokens_ref.shape
    n_group, per_group, packed_width = out_ref.shape
    rows = n_group * per_group
    experts = packed_width - width
    tok = tokens_ref[...].astype(jnp.float32)
    largest = jnp.maximum(jnp.max(jnp.abs(tok), axis=1, keepdims=True), 1e-25)
    power = jnp.floor(jnp.log2(CODE_MAX / largest))
    codes = jnp.round(tok * jnp.exp2(power))
    routes = routes_ref[...]
    gate_codes = jnp.round(gates_ref[...] * GATE_ONE)
    expert = lax.broadcasted_iota(jnp.int32, (count, experts), 1)
    row = lax.broadcasted_iota(jnp.int32, (count, rows), 1)
    token = lax.broadcasted_iota(jnp.int32, (count, rows), 0)
    side = jnp.zeros((count, experts), jnp.float32)
    chosen = jnp.zeros((count, rows), jnp.float32)
    for k in range(routes.shape[1]):
        route = routes[:, k : k + 1]
        side = side + jnp.where(expert == route, gate_codes[:, k : k + 1], 0.0)
        chosen = jnp.where(route // EXP_MESH == row // per_group, 1.0, chosen)
    side = jnp.where(side > 0.0, side, -(power + EXP_BIAS))
    chosen = jnp.where(token // BLOCK == row % per_group, chosen, 0.0)
    chosen = chosen.T.astype(jnp.bfloat16)

    copies = []

    def send(values, first, size):
        high = jnp.floor(values * (1.0 / 256.0))
        low = values - 256.0 * high
        picked = jnp.dot(chosen, (256.0 * high).astype(jnp.bfloat16), preferred_element_type=jnp.float32)
        picked += jnp.dot(chosen, low.astype(jnp.bfloat16), preferred_element_type=jnp.float32)
        picked = picked.astype(jnp.int32).astype(jnp.int16)
        for group in range(n_group):
            staged[group, :, first : first + size] = picked[group * per_group : (group + 1) * per_group]
        cols = pl.ds(first, size)
        copy = pltpu.make_async_copy(staged.at[:, :, cols], out_ref.at[:, :, cols], sent.at[len(copies)])
        copy.start()
        copies.append(copy)

    send(side, width, experts)
    piece = width // CHUNKS
    for chunk in range(CHUNKS):
        send(codes[:, chunk * piece : (chunk + 1) * piece], chunk * piece, piece)
    for copy in copies:
        copy.wait()


def pack_rows(tokens, routes, route_gates, n_group, experts):
    count, width = tokens.shape
    return pl.pallas_call(
        pack_kernel,
        out_shape=jax.ShapeDtypeStruct((n_group, count // BLOCK, width + experts), jnp.int16),
        in_specs=[pl.BlockSpec(memory_space=pltpu.VMEM)] * 3,
        out_specs=pl.BlockSpec(memory_space=pl.ANY),
        scratch_shapes=[
            pltpu.VMEM((n_group, count // BLOCK, width + experts), jnp.int16),
            pltpu.SemaphoreType.DMA((CHUNKS + 1,)),
        ],
    )(tokens, routes, route_gates)


def scale_and_weight(side_ref):
    expert = lax.axis_index("group") * EXP_MESH + lax.axis_index("local") // (lax.axis_size("local") // EXP_MESH)
    side = side_ref[...].astype(jnp.float32)
    lane = lax.broadcasted_iota(jnp.int32, side.shape, 1)
    weight = jnp.sum(jnp.where(lane == expert, jnp.maximum(side, 0.0), 0.0), axis=1, keepdims=True)
    return jnp.exp2(jnp.min(side, axis=1, keepdims=True) + EXP_BIAS), weight * (1.0 / GATE_ONE)


def gated(pre_gate, pre_up, scale, weight, out_ref):
    pre_gate = pre_gate * scale
    out_ref[...] = (pre_gate / (1.0 + jnp.exp(-pre_gate)) * (pre_up * scale) * weight).astype(out_ref.dtype)


def other_kernel(codes_ref, gate_ref, up_hbm, gate_later, up_later, out_ref, rows, held, arrived):
    width = rows.shape[1]
    copy = pltpu.make_async_copy(up_hbm, held, arrived)
    copy.start()
    rows[...] = codes_ref[:, :width].astype(jnp.float32).astype(jnp.bfloat16)
    scale, weight = scale_and_weight(codes_ref.at[:, width:])
    copy.wait()
    pre_gate = jnp.dot(rows[...], gate_ref[...], preferred_element_type=jnp.float32)
    pre_up = jnp.dot(rows[...], held[...], preferred_element_type=jnp.float32)
    gated(pre_gate, pre_up, scale, weight, out_ref)


def own_kernel(codes_ref, rows, gate_ref, up_ref, out_ref):
    scale, weight = scale_and_weight(codes_ref.at[:, rows.shape[1] :])
    pre_gate = jnp.dot(rows[...], gate_ref[...], preferred_element_type=jnp.float32)
    pre_up = jnp.dot(rows[...], up_ref[...], preferred_element_type=jnp.float32)
    gated(pre_gate, pre_up, scale, weight, out_ref)


def hidden_of_other(codes, width, gate, up, gate_later, up_later):
    count = codes.shape[0]
    in_vmem = pl.BlockSpec(memory_space=pltpu.VMEM)
    return pl.pallas_call(
        other_kernel,
        out_shape=[
            jax.ShapeDtypeStruct((count, gate.shape[1]), jnp.bfloat16),
            jax.ShapeDtypeStruct((count, width), jnp.bfloat16),
        ],
        in_specs=[in_vmem, in_vmem, pl.BlockSpec(memory_space=pl.ANY), in_vmem, in_vmem],
        out_specs=[in_vmem, in_vmem],
        scratch_shapes=[pltpu.VMEM(up.shape, up.dtype), pltpu.SemaphoreType.DMA],
        compiler_params=pltpu.CompilerParams(vmem_limit_bytes=16 << 20),
        cost_estimate=pl.CostEstimate(flops=1880000000, bytes_accessed=12000000, transcendentals=131072),
    )(codes, gate, up, gate_later, up_later)


def hidden_of_own(codes, rows, gate, up):
    in_vmem = pl.BlockSpec(memory_space=pltpu.VMEM)
    return pl.pallas_call(
        own_kernel,
        out_shape=jax.ShapeDtypeStruct((rows.shape[0], gate.shape[1]), jnp.bfloat16),
        in_specs=[in_vmem] * 4,
        out_specs=in_vmem,
        compiler_params=pltpu.CompilerParams(vmem_limit_bytes=16 << 20),
        cost_estimate=pl.CostEstimate(flops=1880000000, bytes_accessed=12000000, transcendentals=131072),
    )(codes, rows, gate, up)


def interleave_kernel(own_ref, other_ref, out_ref, staged, ordered, done, sent, *, n_y, per_group):
    in_block = own_ref.shape[0] // n_y
    n_group = in_block // per_group
    per_source = 2 * n_y * per_group
    tiles = own_ref.shape[1] // LANES
    my_core = lax.axis_index("local") % 2
    for lane in range(tiles):
        cols = slice(lane * LANES, (lane + 1) * LANES)
        staged[lane, 0] = own_ref[:, cols].astype(jnp.float32)
        staged[lane, 1] = other_ref[:, cols].astype(jnp.float32)
    groups = n_group // CHUNKS
    copies = []
    for chunk in range(CHUNKS):
        for core in range(2):

            @pl.when(my_core == core)
            def _():
                for lane in range(tiles):
                    for group in range(chunk * groups, (chunk + 1) * groups):
                        for i in range(per_group):
                            origin = pl.ds(group * per_group + i, n_y, stride=in_block)
                            for source in range(2):
                                place = core if source == 0 else 1 - core
                                target = group * per_source + place * per_group + i
                                ordered[lane, pl.ds(target, n_y, stride=2 * per_group), :] = staged[
                                    lane, source, origin, :
                                ]

        rows = slice(chunk * groups * per_source, (chunk + 1) * groups * per_source)
        for lane in range(tiles):
            done[rows, lane * LANES : (lane + 1) * LANES] = ordered[lane, rows].astype(done.dtype)
        copy = pltpu.make_async_copy(done.at[rows], out_ref.at[rows], sent.at[chunk])
        copy.start()
        copies.append(copy)
    for copy in copies:
        copy.wait()


def interleave(own, other, n_y, per_group):
    rows, width = own.shape
    tiles = width // LANES
    return pl.pallas_call(
        functools.partial(interleave_kernel, n_y=n_y, per_group=per_group),
        out_shape=jax.ShapeDtypeStruct((2 * rows, width), own.dtype),
        in_specs=[pl.BlockSpec(memory_space=pltpu.VMEM)] * 2,
        out_specs=pl.BlockSpec(memory_space=pl.ANY),
        scratch_shapes=[
            pltpu.VMEM((tiles, 2, rows, LANES), jnp.float32),
            pltpu.VMEM((tiles, 2 * rows, LANES), jnp.float32),
            pltpu.VMEM((2 * rows, width), own.dtype),
            pltpu.SemaphoreType.DMA((CHUNKS,)),
        ],
        compiler_params=pltpu.CompilerParams(vmem_limit_bytes=8 << 20),
        cost_estimate=pl.CostEstimate(flops=0, bytes_accessed=1000000, transcendentals=0),
    )(own, other)


def shards(tokens, routes, route_gates, gate_weight, up_weight):
    n_group = lax.axis_size("group")
    n_local = lax.axis_size("local")
    n_y = n_local // 2
    width = tokens.shape[1]
    experts = n_group * EXP_MESH
    per_group = tokens.shape[0] // BLOCK
    swap = [(2 * y + c, 2 * y + 1 - c) for y in range(n_y) for c in range(2)]
    same_core = [[2 * y + c for y in range(n_y)] for c in range(2)]

    packed = pack_rows(tokens, routes, route_gates, n_group, experts)
    received = lax.all_to_all(packed, "group", split_axis=0, concat_axis=0, tiled=True)
    other_gate = lax.ppermute(gate_weight, "local", swap)
    other_up = lax.ppermute(up_weight, "local", swap)
    received, other_gate, other_up = lax.optimization_barrier((received, other_gate, other_up))
    received = received.reshape(1, n_group * per_group, width + experts)
    gathered = lax.all_gather(received, "local", axis=0, axis_index_groups=same_core, tiled=True)
    gathered = gathered.reshape(-1, width + experts)

    for_other, rows = hidden_of_other(
        gathered, width, other_gate[0], other_up[0], gate_weight[0], up_weight[0]
    )
    from_other = lax.ppermute(for_other, "local", swap)
    own = hidden_of_own(gathered, rows, gate_weight[0], up_weight[0])
    out = interleave(own, from_other, n_y, per_group)
    return out.reshape((1,) + out.shape)


def solution(mesh):
    placed = (
        P(("group", "local"), None),
        P(("group", "local"), None),
        P(("group", "local"), None),
        P(("group", "local"), None, None),
        P(("group", "local"), None, None),
    )
    return jax.shard_map(
        shards,
        mesh=mesh,
        in_specs=placed,
        out_specs=P(("group", "local"), None, None),
        check_vma=False,
    )
```

```python
import functools

import jax
import jax.numpy as jnp
from jax import lax
from jax.experimental import pallas as pl
from jax.experimental.pallas import tpu as pltpu
from jax.sharding import PartitionSpec as P

EXP_MESH = 4
BLOCK = 4
LANES = 128
CHUNKS = 4
GATE_ONE = 16000.0
CODE_MAX = 32000.0
EXP_BIAS = 200.0


def pack_kernel(tokens_ref, routes_ref, gates_ref, out_ref, staged, sent):
    count, width = tokens_ref.shape
    n_group, per_group, packed_width = out_ref.shape
    rows = n_group * per_group
    experts = packed_width - width
    tok = tokens_ref[...].astype(jnp.float32)
    largest = jnp.maximum(jnp.max(jnp.abs(tok), axis=1, keepdims=True), 1e-25)
    power = jnp.floor(jnp.log2(CODE_MAX / largest))
    codes = jnp.round(tok * jnp.exp2(power))
    routes = routes_ref[...]
    gate_codes = jnp.round(gates_ref[...] * GATE_ONE)
    expert = lax.broadcasted_iota(jnp.int32, (count, experts), 1)
    row = lax.broadcasted_iota(jnp.int32, (count, rows), 1)
    token = lax.broadcasted_iota(jnp.int32, (count, rows), 0)
    side = jnp.zeros((count, experts), jnp.float32)
    chosen = jnp.zeros((count, rows), jnp.float32)
    for k in range(routes.shape[1]):
        route = routes[:, k : k + 1]
        side = side + jnp.where(expert == route, gate_codes[:, k : k + 1], 0.0)
        chosen = jnp.where(route // EXP_MESH == row // per_group, 1.0, chosen)
    side = jnp.where(side > 0.0, side, -(power + EXP_BIAS))
    chosen = jnp.where(token // BLOCK == row % per_group, chosen, 0.0)
    chosen = chosen.T.astype(jnp.bfloat16)

    copies = []

    def send(values, first, size):
        high = jnp.floor(values * (1.0 / 256.0))
        low = values - 256.0 * high
        picked = jnp.dot(chosen, (256.0 * high).astype(jnp.bfloat16), preferred_element_type=jnp.float32)
        picked += jnp.dot(chosen, low.astype(jnp.bfloat16), preferred_element_type=jnp.float32)
        picked = picked.astype(jnp.int32).astype(jnp.int16)
        for group in range(n_group):
            staged[group, :, first : first + size] = picked[group * per_group : (group + 1) * per_group]
        cols = pl.ds(first, size)
        copy = pltpu.make_async_copy(staged.at[:, :, cols], out_ref.at[:, :, cols], sent.at[len(copies)])
        copy.start()
        copies.append(copy)

    send(side, width, experts)
    piece = width // CHUNKS
    for chunk in range(CHUNKS):
        send(codes[:, chunk * piece : (chunk + 1) * piece], chunk * piece, piece)
    for copy in copies:
        copy.wait()


def pack_rows(tokens, routes, route_gates, n_group, experts):
    count, width = tokens.shape
    return pl.pallas_call(
        pack_kernel,
        out_shape=jax.ShapeDtypeStruct((n_group, count // BLOCK, width + experts), jnp.int16),
        in_specs=[pl.BlockSpec(memory_space=pltpu.VMEM)] * 3,
        out_specs=pl.BlockSpec(memory_space=pl.ANY),
        scratch_shapes=[
            pltpu.VMEM((n_group, count // BLOCK, width + experts), jnp.int16),
            pltpu.SemaphoreType.DMA((CHUNKS + 1,)),
        ],
    )(tokens, routes, route_gates)


def scale_and_weight(side_ref):
    expert = lax.axis_index("group") * EXP_MESH + lax.axis_index("local") // (lax.axis_size("local") // EXP_MESH)
    side = side_ref[...].astype(jnp.float32)
    lane = lax.broadcasted_iota(jnp.int32, side.shape, 1)
    weight = jnp.sum(jnp.where(lane == expert, jnp.maximum(side, 0.0), 0.0), axis=1, keepdims=True)
    return jnp.exp2(jnp.min(side, axis=1, keepdims=True) + EXP_BIAS), weight * (1.0 / GATE_ONE)


def gated(pre_gate, pre_up, scale, weight):
    pre_gate = pre_gate * scale
    return pre_gate / (1.0 + jnp.exp(-pre_gate)) * (pre_up * (scale * weight))


def other_kernel(codes_ref, gate_ref, up_hbm, gate_later, up_later, out_ref, rows, held, arrived):
    width = rows.shape[1]
    copy = pltpu.make_async_copy(up_hbm, held, arrived)
    copy.start()
    rows[...] = codes_ref[:, :width].astype(jnp.float32).astype(jnp.bfloat16)
    copy.wait()
    scale, weight = scale_and_weight(codes_ref.at[:, width:])
    pre_gate = jnp.dot(rows[...], gate_ref[...], preferred_element_type=jnp.float32)
    pre_up = jnp.dot(rows[...], held[...], preferred_element_type=jnp.float32)
    out_ref[...] = gated(pre_gate, pre_up, scale, weight).astype(out_ref.dtype)


def own_kernel(codes_ref, rows, gate_ref, up_ref, out_ref):
    scale, weight = scale_and_weight(codes_ref.at[:, rows.shape[1] :])
    pre_gate = jnp.dot(rows[...], gate_ref[...], preferred_element_type=jnp.float32)
    pre_up = jnp.dot(rows[...], up_ref[...], preferred_element_type=jnp.float32)
    own = gated(pre_gate, pre_up, scale, weight)
    for lane in range(out_ref.shape[0]):
        out_ref[lane] = own[:, lane * LANES : (lane + 1) * LANES]


def hidden_of_other(codes, width, gate, up, gate_later, up_later):
    count = codes.shape[0]
    in_vmem = pl.BlockSpec(memory_space=pltpu.VMEM)
    return pl.pallas_call(
        other_kernel,
        out_shape=[
            jax.ShapeDtypeStruct((count, gate.shape[1]), jnp.bfloat16),
            jax.ShapeDtypeStruct((count, width), jnp.bfloat16),
        ],
        in_specs=[in_vmem, in_vmem, pl.BlockSpec(memory_space=pl.ANY), in_vmem, in_vmem],
        out_specs=[in_vmem, in_vmem],
        scratch_shapes=[pltpu.VMEM(up.shape, up.dtype), pltpu.SemaphoreType.DMA],
        compiler_params=pltpu.CompilerParams(vmem_limit_bytes=16 << 20),
        cost_estimate=pl.CostEstimate(flops=1880000000, bytes_accessed=12000000, transcendentals=131072),
    )(codes, gate, up, gate_later, up_later)


def hidden_of_own(codes, rows, gate, up):
    in_vmem = pl.BlockSpec(memory_space=pltpu.VMEM)
    return pl.pallas_call(
        own_kernel,
        out_shape=jax.ShapeDtypeStruct((gate.shape[1] // LANES, rows.shape[0], LANES), jnp.float32),
        in_specs=[in_vmem] * 4,
        out_specs=in_vmem,
        compiler_params=pltpu.CompilerParams(vmem_limit_bytes=16 << 20),
        cost_estimate=pl.CostEstimate(flops=1880000000, bytes_accessed=12000000, transcendentals=131072),
    )(codes, rows, gate, up)


def interleave_kernel(own_ref, other_ref, out_ref, staged, ordered, done, sent, *, n_y, per_group):
    in_block = own_ref.shape[1] // n_y
    n_group = in_block // per_group
    per_source = 2 * n_y * per_group
    tiles = own_ref.shape[0]
    my_core = lax.axis_index("local") % 2
    for lane in range(tiles):
        cols = slice(lane * LANES, (lane + 1) * LANES)
        staged[lane] = other_ref[:, cols].astype(jnp.float32)
    groups = n_group // CHUNKS
    copies = []
    for chunk in range(CHUNKS):
        for core in range(2):

            @pl.when(my_core == core)
            def _():
                for lane in range(tiles):
                    for group in range(chunk * groups, (chunk + 1) * groups):
                        for i in range(per_group):
                            origin = pl.ds(group * per_group + i, n_y, stride=in_block)
                            for source, place in ((own_ref, core), (staged, 1 - core)):
                                target = group * per_source + place * per_group + i
                                ordered[lane, pl.ds(target, n_y, stride=2 * per_group), :] = source[lane, origin, :]

        rows = slice(chunk * groups * per_source, (chunk + 1) * groups * per_source)
        for lane in range(tiles):
            done[rows, lane * LANES : (lane + 1) * LANES] = ordered[lane, rows].astype(done.dtype)
        copy = pltpu.make_async_copy(done.at[rows], out_ref.at[rows], sent.at[chunk])
        copy.start()
        copies.append(copy)
    for copy in copies:
        copy.wait()


def interleave(own, other, n_y, per_group):
    tiles, rows, _ = own.shape
    width = tiles * LANES
    return pl.pallas_call(
        functools.partial(interleave_kernel, n_y=n_y, per_group=per_group),
        out_shape=jax.ShapeDtypeStruct((2 * rows, width), other.dtype),
        in_specs=[pl.BlockSpec(memory_space=pltpu.VMEM)] * 2,
        out_specs=pl.BlockSpec(memory_space=pl.ANY),
        scratch_shapes=[
            pltpu.VMEM((tiles, rows, LANES), jnp.float32),
            pltpu.VMEM((tiles, 2 * rows, LANES), jnp.float32),
            pltpu.VMEM((2 * rows, width), other.dtype),
            pltpu.SemaphoreType.DMA((CHUNKS,)),
        ],
        compiler_params=pltpu.CompilerParams(vmem_limit_bytes=8 << 20),
        cost_estimate=pl.CostEstimate(flops=0, bytes_accessed=1000000, transcendentals=0),
    )(own, other)


def shards(tokens, routes, route_gates, gate_weight, up_weight):
    n_group = lax.axis_size("group")
    n_local = lax.axis_size("local")
    n_y = n_local // 2
    width = tokens.shape[1]
    experts = n_group * EXP_MESH
    per_group = tokens.shape[0] // BLOCK
    swap = [(2 * y + c, 2 * y + 1 - c) for y in range(n_y) for c in range(2)]
    same_core = [[2 * y + c for y in range(n_y)] for c in range(2)]

    packed = pack_rows(tokens, routes, route_gates, n_group, experts)
    received = lax.all_to_all(packed, "group", split_axis=0, concat_axis=0, tiled=True)
    other_gate = lax.ppermute(gate_weight, "local", swap)
    other_up = lax.ppermute(up_weight, "local", swap)
    received, other_gate = lax.optimization_barrier((received, other_gate))
    received = received.reshape(1, n_group * per_group, width + experts)
    gathered = lax.all_gather(received, "local", axis=0, axis_index_groups=same_core, tiled=True)
    gathered = gathered.reshape(-1, width + experts)

    for_other, rows = hidden_of_other(
        gathered, width, other_gate[0], other_up[0], gate_weight[0], up_weight[0]
    )
    from_other = lax.ppermute(for_other, "local", swap)
    own = hidden_of_own(gathered, rows, gate_weight[0], up_weight[0])
    out = interleave(own, from_other, n_y, per_group)
    return out.reshape((1,) + out.shape)


def solution(mesh):
    placed = (
        P(("group", "local"), None),
        P(("group", "local"), None),
        P(("group", "local"), None),
        P(("group", "local"), None, None),
        P(("group", "local"), None, None),
    )
    return jax.shard_map(
        shards,
        mesh=mesh,
        in_specs=placed,
        out_specs=P(("group", "local"), None, None),
        check_vma=False,
    )
```
